32 devices in a mesh: rows: 16 (over z, y, x), cols: 2 (over core).
Axes of the slice: x: 2, y: 2, z: 4, core: 2. Of those that a mesh axis runs over, the one named last changes fastest.
Arguments:
- descriptors: bfloat16 [4096, 1024], P(('rows', 'cols')), may hold values from -6 to 6
- sparse_points: bfloat16 [8192, 1024], P('cols'), may hold values from -6 to 6
- point_scale: float32 [8192], P('cols'), may hold values from 0.3 to 3
- env_owner: int32 [4096, 1], P('rows'), may hold values from 0 to 15; in each aligned block of 128 rows (0 to 127, 128 to 255, ...) at most 12 rows name the same one
- env_structure: int32 [4096], P('rows'), may hold values from 0 to 63
- row_weight: float32 [1024], P('rows'), may hold values from 0.01 to 0.1
- ridge_factor: float32 [1], replicated, may hold values from 0.05 to 0.5
Outputs:
- r_rows: float32 [128, 8192], P(None, 'cols')
- reduced: float32 [1024, 8192], P('rows', 'cols')
The draws below stay inside these ranges and needn't reach their ends.
Inputs may be any that keep to these rules, and one draw needn't show every extreme that they name: `env_owner`: in each aligned block of 128 environments, no owner is named by more than 12 of them.
All inputs are finite; a program needn't handle non-finite values.
Results may differ from the reference program's by a relative error of at most 0.0045.
Values may be sent and summed in bfloat16 or wider, within the bound.
A program may use at most 64 MiB of HBM per device.

```python
import math
import jax
import jax.numpy as jnp
import numpy as np
from jax import lax

DESC = 1024
M = 8192
PW = 64
PANELS = 2
ENV_DEV = 256
EQ_DEV = 64
HALF = 128
CAP = 12
ENV = 4096
NEQ = 1024
N_ROWS = 16


def plant(result, key, least, top_value):
    place = [jax.random.randint(jax.random.fold_in(key, axis), (), 0, length) for axis, length in enumerate(result.shape)]
    widest = result.shape.index(max(result.shape))
    beside = place[:widest] + [(place[widest] + 1) % result.shape[widest]] + place[widest + 1:]
    return result.at[tuple(place)].set(least).at[tuple(beside)].set(top_value)


def level_of(own_key, dims, cuts, low, largest):
    def one(axis_at, parts):
        steps = jax.random.uniform(jax.random.fold_in(jax.random.fold_in(own_key, 6), axis_at), (parts,), jnp.float32, low / len(cuts), largest / len(cuts))
        return jnp.repeat(jnp.exp(steps), dims[axis_at] // parts).reshape((-1,) + (1,) * (len(dims) - axis_at - 1))

    level = one(*cuts[0])
    for cut in cuts[1:]:
        level = level * one(*cut)
    return level


def deal_out(key, own, number, rows, number_of, top, bound, skew):
    ranking = jax.random.permutation(key, number_of)
    crowded, common = shares(number_of, rows * top, bound, skew, True), shares(number_of, rows * top, bound, skew, False)
    places = jnp.arange(number_of)

    def named(lengths, turn):
        used = int((lengths > 0).sum())
        fixed = max(1, used // 4)
        passed = fixed + (places - fixed + turn * (used - fixed)) % max(1, number_of - fixed)
        return jnp.zeros((number_of,), jnp.int32).at[ranking[jnp.where(places < fixed, places, passed)]].set(jnp.asarray(lengths, jnp.int32))

    lengths = jnp.where(number % 4 == 0, named(crowded, number // 4), named(common, number - number // 4 - 1))
    mixed = jax.random.permutation(jax.random.fold_in(own, 3), number_of)
    source_of, sink = mixed[0:number_of // 2 * 2:2], mixed[1:number_of // 2 * 2:2]
    room = jnp.minimum(lengths[source_of] - 1, bound - lengths[sink]) // 2
    room = jnp.where((source_of == ranking[0]) | (sink == ranking[0]) | (lengths[sink] == 0), 0, jnp.maximum(room, 0))
    passed = jax.random.randint(jax.random.fold_in(own, 4), (number_of // 2,), 0, 1 << 20) % (room + 1)
    lengths = lengths.at[source_of].add(-passed).at[sink].add(passed)
    items = jnp.searchsorted(jnp.cumsum(lengths), jnp.arange(rows * top), side="right").astype(jnp.int32)
    grid = items.reshape(top, rows).T
    grid = grid[jax.random.permutation(jax.random.fold_in(own, 1), rows)]
    turn = jax.random.randint(jax.random.fold_in(own, 2), (rows, 1), 0, top)
    return jnp.take_along_axis(grid, (jnp.arange(top)[None, :] + turn) % top, axis=1)


def shares(amount, total, bound, skew, full):
    weights = [(1 << 20) // math.isqrt(rank ** skew) + 1 for rank in range(1, amount + 1)]
    largest = bound if full else min(bound, max(-(-total // amount), total * weights[0] // sum(weights)))
    least = 1 if total - largest >= amount - 1 else 0
    counts, rest = [largest] + [least] * (amount - 1), total - largest - least * (amount - 1)
    while rest > 0:
        free = [i for i in range(1, amount) if counts[i] < largest] or [i for i in range(1, amount) if counts[i] < bound]
        pool, left = sum([weights[i] for i in free]), rest
        for i in free:
            extra = min(bound - counts[i], max(1, left * weights[i] // pool), rest)
            counts[i] = counts[i] + extra
            rest = rest - extra
    return np.array(counts)


def scatter_about(stream_key, shape, scale, reach, shards=(), kind=jnp.bfloat16):
    array = jax.random.normal(stream_key, shape, jnp.float32) * scale
    if len(shards) > 0:
        array = level_of(stream_key, shape, shards, -0.22, 0.18) * array
    return jnp.clip(array, min=-reach, max=reach).astype(kind)


def setup_inputs(seed: int = 0) -> dict:
    key_list = jax.random.split(jax.random.key(seed), 8)
    descriptors = scatter_about(key_list[0], (ENV, DESC), 1.0, 6.0, ((0, 32),))
    sparse_points = scatter_about(key_list[1], (M, DESC), 1.0, 6.0, ((0, 2),))
    point_scale = jnp.clip(jnp.exp(math.log(3.0) - 2.3025851 * jax.random.uniform(key_list[2], (M,), jnp.float32) ** level_of(key_list[2], (M,), ((0, 2),), -0.2, 0.2)), 0.3, 3.0)
    env_owner_keys = jax.random.split(jax.random.fold_in(key_list[3], 1), ENV // HALF)
    env_owner_turns = jax.random.permutation(jax.random.fold_in(key_list[3], 3), ENV // HALF)
    env_owner = jax.vmap(lambda own, number: deal_out(jax.random.fold_in(key_list[3], 2), own, number, HALF, N_ROWS, 1, CAP, 2))(env_owner_keys, env_owner_turns).reshape((ENV, 1))
    env_structure = plant(jax.random.randint(key_list[4], (ENV,), 0, EQ_DEV), jax.random.fold_in(key_list[4], 1), 0, EQ_DEV - 1).astype(jnp.int32)
    row_weight = jnp.clip(jnp.exp(math.log(0.1) - 2.3025851 * jax.random.uniform(key_list[5], (NEQ,), jnp.float32) ** level_of(key_list[5], (NEQ,), ((0, 16),), -0.2, 0.2)), 0.01, 0.1)
    ridge_factor = jnp.clip(jnp.exp(jax.random.uniform(key_list[6], (1,), jnp.float32, math.log(0.05), math.log(0.5))), 0.05, 0.5)
    return {"descriptors": descriptors, "sparse_points": sparse_points, "point_scale": point_scale, "env_owner": env_owner, "env_structure": env_structure, "row_weight": row_weight, "ridge_factor": ridge_factor}


def inner_cols(left, right):
    return lax.dot_general(left.astype(jnp.float32), right.astype(jnp.float32), (((0,), (0,)), ((), ())), precision=lax.Precision.HIGHEST, preferred_element_type=jnp.float32)

def factor(gram_mat, ridge_factor):
    shift = ridge_factor[0] * jnp.trace(gram_mat) / PW + 1e-06
    chol_lower = jnp.linalg.cholesky(gram_mat + shift * jnp.eye(PW, dtype=jnp.float32))
    inverse = jax.scipy.linalg.solve_triangular(chol_lower, jnp.eye(PW, dtype=jnp.float32), lower=True)
    return (chol_lower, inverse)

def reference(descriptors, sparse_points, point_scale, env_owner, env_structure, row_weight, ridge_factor):
    dot_scale = DESC ** (-0.5)
    points = sparse_points.astype(jnp.float32)
    global_ids = (env_owner[:, 0].astype(jnp.int32) * EQ_DEV + env_structure.astype(jnp.int32)).astype(jnp.int32)
    desc_blocks = descriptors.reshape(N_ROWS, ENV_DEV, DESC)
    id_blocks = global_ids.reshape(N_ROWS, ENV_DEV)

    def add_block(sums, pieces):
        env_rows, env_ids = pieces
        products = jnp.dot(env_rows.astype(jnp.float32), points.T.astype(jnp.float32), precision=lax.Precision.HIGHEST, preferred_element_type=jnp.float32) * dot_scale
        squared = products * products
        kernel = (point_scale[None, :] * squared * squared).astype(jnp.bfloat16)
        kernel = lax.optimization_barrier(kernel).astype(jnp.float32)
        return (sums + jax.ops.segment_sum(kernel, env_ids, num_segments=NEQ), None)
    sums, _ = lax.scan(add_block, jnp.zeros((NEQ, M), jnp.float32), (desc_blocks, id_blocks))
    matrix = sums * row_weight[:, None]
    col_ids = jnp.arange(M, dtype=jnp.int32)[None, :]
    norm_scale = 1.0 / NEQ ** 0.5
    r_blocks = []
    for panel_idx in range(PANELS):
        first_col = panel_idx * PW
        panel_cols = matrix[:, first_col:first_col + PW]
        chol_lower, inverse = factor(inner_cols(panel_cols, panel_cols), ridge_factor)
        q_cols = jnp.dot(panel_cols.astype(jnp.float32), inverse.T.astype(jnp.float32), precision=lax.Precision.HIGHEST, preferred_element_type=jnp.float32)
        coupled = inner_cols(q_cols, matrix)
        later_mask = col_ids >= first_col + PW
        inside = (col_ids >= first_col) & (col_ids < first_col + PW)
        coupled = jnp.where(later_mask, coupled, 0.0)
        update = jnp.dot(q_cols.astype(jnp.float32), coupled.astype(jnp.float32), precision=lax.Precision.HIGHEST, preferred_element_type=jnp.float32)
        q_wide = jnp.pad(q_cols, ((0, 0), (first_col, M - first_col - PW)))
        matrix = jnp.where(inside, q_wide, matrix - update)
        r_wide = jnp.pad(chol_lower.T, ((0, 0), (first_col, M - first_col - PW)))
        r_blocks.append(jnp.where(inside, r_wide, coupled) * norm_scale)
    return (jnp.concatenate(r_blocks, axis=0), matrix)
```

```python
import math

import jax
import jax.numpy as jnp
from jax import lax
from jax.sharding import PartitionSpec as P

PW = 64
PANELS = 2
BLOCK = 128
LANES = 128
HI = lax.Precision.HIGHEST
F32 = jnp.float32


def mm(left, right, contract, precision=HI):
    return lax.dot_general(
        left, right, ((contract[0], contract[1]), ((), ())), precision=precision,
        preferred_element_type=F32,
    )


def from_root(value, axis):
    return lax.all_gather(value, axis)[0]


def kernel_rows(env_rows, points, scale):
    products = mm(env_rows, points, ((1,), (1,)), None) * env_rows.shape[1] ** (-0.5)
    squared = products * products
    return (scale[None, :] * squared * squared).astype(jnp.bfloat16)


def spread(value, axis):
    size = lax.axis_size(axis)
    return lax.all_to_all(
        jnp.broadcast_to(value[None], (size,) + value.shape), axis, 0, 0, tiled=True
    )


def factor(gram_mat, ridge_factor):
    eye = jnp.eye(PW, dtype=F32)
    shift = ridge_factor[0] * jnp.trace(gram_mat) / PW + 1e-06
    chol_lower = jnp.linalg.cholesky(gram_mat + shift * eye)
    return chol_lower, jax.scipy.linalg.solve_triangular(chol_lower, eye, lower=True)


def body(
    descriptors, sparse_points, point_scale, env_owner, env_structure, row_weight, ridge_factor
):
    owners = lax.axis_size("rows")
    col_index = lax.axis_index("cols")
    eq_count = row_weight.shape[0]
    env_local, desc = descriptors.shape
    wide = PANELS * PW

    head_points = from_root(sparse_points[:wide], "cols")
    head_scale = from_root(point_scale[:wide], "cols")

    per_block = max(2, (3 * BLOCK + 2 * owners - 1) // (2 * owners))
    capacity = min(env_local, per_block * (-(-env_local // BLOCK)))
    own = lax.dynamic_slice_in_dim(env_owner[:, 0], col_index * env_local, env_local)
    struct = lax.dynamic_slice_in_dim(env_structure, col_index * env_local, env_local)
    idx = jnp.arange(env_local)
    within = jnp.sum(
        ((own[:, None] == own[None, :]) & (idx[None, :] < idx[:, None])).astype(jnp.int32), axis=1
    )
    slot = own * capacity + within
    slots = lax.broadcasted_iota(jnp.int32, (owners * capacity, env_local), 0)
    pick = (slots == slot[None, :]).astype(jnp.bfloat16)
    lane = lax.broadcasted_iota(jnp.int32, (env_local, LANES), 1)
    tag = jnp.where(lane == 0, struct[:, None] + 1, 0).astype(jnp.bfloat16)
    payload = mm(
        pick, jnp.concatenate([descriptors, tag], axis=1), ((1,), (0,)), None
    ).astype(jnp.bfloat16)
    arrived = lax.all_to_all(payload, "rows", 0, 0, tiled=True)
    arrived = lax.all_gather(arrived, "cols", axis=0, tiled=True)
    env_rows = arrived[:, :desc]
    labels = arrived[:, desc].astype(jnp.int32) - 1
    targets = lax.broadcasted_iota(jnp.int32, (eq_count, labels.shape[0]), 0)
    selector = (labels[None, :] == targets).astype(jnp.bfloat16)

    def equations(points, scale):
        kernel = kernel_rows(env_rows, points, scale)
        return mm(selector, kernel, ((1,), (0,)), None) * row_weight[:, None]

    head = equations(head_points, head_scale)
    head_all = spread(head, "rows").reshape(owners * eq_count, wide)
    matrix = equations(sparse_points, point_scale)
    col_count = matrix.shape[1]

    part = col_count // owners
    cross = mm(head, matrix, ((0,), (0,)))
    cross = cross.reshape(wide, owners, part).transpose(1, 0, 2).astype(jnp.bfloat16)
    cross = lax.all_to_all(cross, "rows", 0, 0, tiled=True)
    cross = jnp.sum(cross.astype(F32), axis=0)

    gram = mm(head_all, head_all, ((0,), (0,)))
    low1, inv1 = factor(gram[:PW, :PW], ridge_factor)
    c12 = mm(inv1, gram[:PW, PW:], ((1,), (0,)))
    overlap = mm(mm(inv1, gram[:PW, :PW], ((1,), (0,))), inv1, ((1,), (1,)))
    twice = 2.0 * jnp.eye(PW, dtype=F32) - overlap
    mixed = mm(c12, twice, ((0,), (0,)))
    low2, inv2 = factor(gram[PW:, PW:] - mm(mixed, c12, ((1,), (0,))), ridge_factor)
    q1 = mm(head[:, :PW], inv1, ((1,), (1,)))
    q2 = mm(head[:, PW:] - mm(q1, c12, ((1,), (0,))), inv2, ((1,), (1,)))

    c1 = mm(inv1, cross[:PW], ((1,), (0,)))
    c2 = mm(inv2, cross[PW:] - mm(mixed, c1, ((1,), (0,))), ((1,), (0,)))
    coupled = spread(jnp.concatenate([c1, c2], axis=0).astype(jnp.bfloat16), "rows")
    coupled = coupled.transpose(1, 0, 2).reshape(wide, col_count).astype(F32)

    q_cols = jnp.concatenate([q1, q2], axis=1)
    update = mm(q_cols, coupled, ((1,), (0,)))
    norm_scale = 1.0 / math.sqrt(owners * eq_count)
    zero = jnp.zeros((PW, PW), F32)
    r_head = jnp.concatenate(
        [jnp.concatenate([low1.T, c12], axis=1), jnp.concatenate([zero, low2.T], axis=1)], axis=0
    )
    root = col_index == 0
    reduced = matrix - update
    reduced_head = jnp.where(root, q_cols, reduced[:, :wide])
    r_head = jnp.where(root, r_head, coupled[:, :wide])
    reduced = jnp.concatenate([reduced_head, reduced[:, wide:]], axis=1)
    r_rows = jnp.concatenate([r_head, coupled[:, wide:]], axis=1) * norm_scale
    return r_rows, reduced


def solution(mesh):
    return jax.shard_map(
        body,
        mesh=mesh,
        in_specs=(
            P(("rows", "cols"), None),
            P("cols", None),
            P("cols"),
            P("rows", None),
            P("rows"),
            P("rows"),
            P(),
        ),
        out_specs=(P(None, "cols"), P("rows", "cols")),
        check_vma=False,
    )
```

```python
import math

import jax
import jax.numpy as jnp
from jax import lax
from jax.experimental import pallas as pl
from jax.experimental.pallas import tpu as pltpu
from jax.sharding import PartitionSpec as P

PW = 64
PANELS = 2
BLOCK = 128
LANES = 128
HI = lax.Precision.HIGHEST
F32 = jnp.float32


def mm(left, right, contract, precision=HI):
    return lax.dot_general(
        left, right, ((contract[0], contract[1]), ((), ())), precision=precision,
        preferred_element_type=F32,
    )


def from_root(value, axis):
    return lax.all_gather(value, axis)[0]


def kernel_rows(env_rows, points, scale):
    products = mm(env_rows, points, ((1,), (1,)), None) * env_rows.shape[1] ** (-0.5)
    squared = products * products
    return (scale[None, :] * squared * squared).astype(jnp.bfloat16)


def spread(value, axis):
    size = lax.axis_size(axis)
    return lax.all_to_all(
        jnp.broadcast_to(value[None], (size,) + value.shape), axis, 0, 0, tiled=True
    )


def eliminate(in_ref, out_ref):
    work = in_ref[...]
    rows = lax.broadcasted_iota(jnp.int32, work.shape, 0)
    lanes = lax.broadcasted_iota(jnp.int32, work.shape, 1)
    for k in range(PW):
        ratio = work[:, k : k + 1] / work[k : k + 1, k : k + 1]
        work = work - jnp.where(rows > k, ratio * work[k : k + 1, :], 0.0)
    pivots = jnp.sum(jnp.where(lanes == rows, work, 0.0), axis=1, keepdims=True)
    out_ref[...] = jnp.where(lanes < rows, 0.0, work / jnp.sqrt(pivots))


def factor(gram_mat, ridge_factor):
    eye = jnp.eye(PW, dtype=F32)
    shift = ridge_factor[0] * jnp.trace(gram_mat) / PW + 1e-06
    both = pl.pallas_call(
        eliminate,
        out_shape=jax.ShapeDtypeStruct((PW, 2 * PW), F32),
        in_specs=[pl.BlockSpec(memory_space=pltpu.VMEM)],
        out_specs=pl.BlockSpec(memory_space=pltpu.VMEM),
        cost_estimate=pl.CostEstimate(flops=8000000, bytes_accessed=65536, transcendentals=0),
    )(jnp.concatenate([gram_mat + shift * eye, eye], axis=1))
    return both[:, :PW], both[:, PW:]


def body(
    descriptors, sparse_points, point_scale, env_owner, env_structure, row_weight, ridge_factor
):
    owners = lax.axis_size("rows")
    col_index = lax.axis_index("cols")
    eq_count = row_weight.shape[0]
    env_local, desc = descriptors.shape
    wide = PANELS * PW

    head_points = from_root(sparse_points[:wide], "cols")
    head_scale = from_root(point_scale[:wide], "cols")

    per_block = max(2, (3 * BLOCK + 2 * owners - 1) // (2 * owners))
    capacity = min(env_local, per_block * (-(-env_local // BLOCK)))
    own = lax.dynamic_slice_in_dim(env_owner[:, 0], col_index * env_local, env_local)
    struct = lax.dynamic_slice_in_dim(env_structure, col_index * env_local, env_local)
    idx = jnp.arange(env_local)
    within = jnp.sum(
        ((own[:, None] == own[None, :]) & (idx[None, :] < idx[:, None])).astype(jnp.int32), axis=1
    )
    slot = own * capacity + within
    slots = lax.broadcasted_iota(jnp.int32, (owners * capacity, env_local), 0)
    pick = (slots == slot[None, :]).astype(jnp.bfloat16)
    lane = lax.broadcasted_iota(jnp.int32, (env_local, LANES), 1)
    tag = jnp.where(lane == 0, struct[:, None] + 1, 0).astype(jnp.bfloat16)
    payload = mm(
        pick, jnp.concatenate([descriptors, tag], axis=1), ((1,), (0,)), None
    ).astype(jnp.bfloat16)
    arrived = lax.all_to_all(payload, "rows", 0, 0, tiled=True)
    arrived = lax.all_gather(arrived, "cols", axis=0, tiled=True)
    env_rows = arrived[:, :desc]
    labels = arrived[:, desc].astype(jnp.int32) - 1
    targets = lax.broadcasted_iota(jnp.int32, (eq_count, labels.shape[0]), 0)
    selector = (labels[None, :] == targets).astype(jnp.bfloat16)

    def equations(points, scale):
        kernel = kernel_rows(env_rows, points, scale)
        return mm(selector, kernel, ((1,), (0,)), None) * row_weight[:, None]

    head = equations(head_points, head_scale)
    head_all = spread(head, "rows").reshape(owners * eq_count, wide)
    matrix = equations(sparse_points, point_scale)
    col_count = matrix.shape[1]

    part = col_count // owners
    level = head_scale / jnp.sum(head_scale * head_scale)
    along = jnp.sum(head * level[None, :], axis=1, keepdims=True)
    rest = head - along * head_scale[None, :]
    cross = mm(rest, matrix, ((0,), (0,)))
    lead = mm(along, matrix, ((0,), (0,)))
    lead_top = lax.reduce_precision(lead, 8, 7)
    pad = jnp.zeros((14, col_count), F32)
    sent = jnp.concatenate([cross, lead_top, lead - lead_top, pad], axis=0)
    sent = sent.reshape(wide + 16, owners, part).transpose(1, 0, 2).astype(jnp.bfloat16)
    sent = lax.all_to_all(sent, "rows", 0, 0, tiled=True)
    sent = jnp.sum(sent.astype(F32), axis=0)
    cross = sent[:wide] + head_scale[:, None] * (sent[wide] + sent[wide + 1])[None, :]

    gram = mm(head_all, head_all, ((0,), (0,)))
    up1, inv1 = factor(gram[:PW, :PW], ridge_factor)
    c12 = mm(inv1, gram[:PW, PW:], ((1,), (0,)))
    overlap = mm(mm(inv1, gram[:PW, :PW], ((1,), (0,))), inv1, ((1,), (1,)))
    twice = 2.0 * jnp.eye(PW, dtype=F32) - overlap
    mixed = mm(c12, twice, ((0,), (0,)))
    up2, inv2 = factor(gram[PW:, PW:] - mm(mixed, c12, ((1,), (0,))), ridge_factor)
    q1 = mm(head[:, :PW], inv1, ((1,), (1,)))
    q2 = mm(head[:, PW:] - mm(q1, c12, ((1,), (0,))), inv2, ((1,), (1,)))

    c1 = mm(inv1, cross[:PW], ((1,), (0,)))
    c2 = mm(inv2, cross[PW:] - mm(mixed, c1, ((1,), (0,))), ((1,), (0,)))
    coupled = spread(jnp.concatenate([c1, c2], axis=0).astype(jnp.bfloat16), "rows")
    coupled = coupled.transpose(1, 0, 2).reshape(wide, col_count).astype(F32)

    q_cols = jnp.concatenate([q1, q2], axis=1)
    update = mm(q_cols, coupled, ((1,), (0,)))
    norm_scale = 1.0 / math.sqrt(owners * eq_count)
    zero = jnp.zeros((PW, PW), F32)
    r_head = jnp.concatenate(
        [jnp.concatenate([up1, c12], axis=1), jnp.concatenate([zero, up2], axis=1)], axis=0
    )
    root = col_index == 0
    reduced = matrix - update
    reduced_head = jnp.where(root, q_cols, reduced[:, :wide])
    r_head = jnp.where(root, r_head, coupled[:, :wide])
    reduced = jnp.concatenate([reduced_head, reduced[:, wide:]], axis=1)
    r_rows = jnp.concatenate([r_head, coupled[:, wide:]], axis=1) * norm_scale
    return r_rows, reduced


def solution(mesh):
    return jax.shard_map(
        body,
        mesh=mesh,
        in_specs=(
            P(("rows", "cols"), None),
            P("cols", None),
            P("cols"),
            P("rows", None),
            P("rows"),
            P("rows"),
            P(),
        ),
        out_specs=(P(None, "cols"), P("rows", "cols")),
        check_vma=False,
    )
```
